32 devices in a mesh: band: 8 (over z, x), grid: 4 (over y, core).
Axes of the slice: x: 2, y: 2, z: 4, core: 2. Of those that a mesh axis runs over, the one named last changes fastest.
Arguments:
- bands: float32 [16, 96, 96, 96], P('band', 'grid'), may hold values from -6 to 6
Outputs:
- exchange_out: float32 [16, 96, 96, 96], P('band', 'grid')
The draws below stay inside these ranges and needn't reach their ends.
All inputs are finite; a program needn't handle non-finite values.
Results may differ from the reference program's by a relative error of at most 0.0091.
Values may be sent and summed in bfloat16 or wider, within the bound.
A program may use at most 128 MiB of HBM per device.

```python
import jax
import jax.numpy as jnp
import numpy as np
from jax import lax

NG = 96
BD = 2
ROUNDS = 3
BLOCKS = 8
NBANDS = 16


def shard_levels(stream_key, extent, split, least, largest):
    level, own = 1.0, jax.random.fold_in(stream_key, 6)
    for dim, parts in split:
        draws = jnp.exp(jax.random.uniform(jax.random.fold_in(own, dim), (parts,), jnp.float32, least / len(split), largest / len(split)))
        level = level * jnp.repeat(draws, extent[dim] // parts).reshape([-1 if axis == dim else 1 for axis in range(len(extent))])
    return level


def bell_draw(own_key, dims, width, reach, split=(), kind=jnp.bfloat16):
    array = width * jax.random.normal(own_key, dims, jnp.float32)
    if split:
        array = array * shard_levels(own_key, dims, split, -0.22, 0.18)
    return jnp.clip(array, -reach, reach).astype(kind)


def setup_inputs(seed: int = 0) -> dict:
    keys = jax.random.split(jax.random.key(seed), 2)
    return {
        "bands": bell_draw(keys[0], (NBANDS, NG, NG, NG), 1.0, 6.0, ((0, 8), (1, 4)), jnp.float32),
    }


kernel_scale = 16.0
screen_sq = 0.05


def dft_table(length):
    half = length // 2
    rows = np.arange(length)
    freq = np.where(rows <= half, rows, rows - half)
    phase = 2.0 * np.pi * np.outer(freq, rows) / length
    return np.where((rows <= half)[:, None], np.cos(phase), np.sin(phase))


def frequency_weights(rows, length):
    half = length // 2
    freq = jnp.where(rows <= half, rows, rows - half).astype(jnp.float32)
    weight = jnp.where((rows == 0) | (rows == half), 1.0, 2.0).astype(jnp.float32) / length
    return freq, weight


def multiplier(rows_x, rows_y, rows_z, length):
    freq_x, weight_x = frequency_weights(rows_x, length)
    freq_y, weight_y = frequency_weights(rows_y, length)
    freq_z, weight_z = frequency_weights(rows_z, length)
    square = freq_x[:, None, None] ** 2 + freq_y[None, :, None] ** 2 + freq_z[None, None, :] ** 2
    scale = weight_x[:, None, None] * weight_y[None, :, None] * weight_z[None, None, :]
    return kernel_scale * scale / (square + screen_sq)


def apply_table(form, cosines, data):
    return jnp.einsum(form, cosines.astype(jnp.float32), data.astype(jnp.float32), precision=lax.Precision.HIGHEST)


def potential_of(density, cosines, weights):
    section_one = apply_table("cz,pxyz->pxyc", cosines, density).astype(jnp.bfloat16)
    section_two = apply_table("cy,pxyz->pxcz", cosines, section_one).astype(jnp.bfloat16)
    section_three = (weights[None] * apply_table("cx,pxyz->pcyz", cosines, section_two)).astype(jnp.bfloat16)
    section_four = apply_table("cx,pcyz->pxyz", cosines, section_three).astype(jnp.bfloat16)
    section_five = apply_table("cy,pxcz->pxyz", cosines, section_four).astype(jnp.bfloat16)
    return apply_table("cz,pxyc->pxyz", cosines, section_five).astype(jnp.bfloat16)


def reference(bands):
    length = bands.shape[1]
    copies = bands.astype(jnp.bfloat16).reshape(BLOCKS, BD, length, length, length)
    cosines = jnp.asarray(dft_table(length), jnp.bfloat16)
    indices = jnp.arange(length, dtype=jnp.int32)
    weights = multiplier(indices, indices, indices, length)
    summed = jnp.zeros((BLOCKS, BD, length, length, length), jnp.float32)
    for round_index in range(1, ROUNDS + 1):
        partners = jnp.roll(copies, round_index, axis=0)

        def one_block(pair_blocks):
            mine, other = pair_blocks
            density = (mine[:, None].astype(jnp.float32) * other[None].astype(jnp.float32)).astype(jnp.bfloat16)
            density = density.reshape(BD * BD, length, length, length)
            field = potential_of(density, cosines, weights).reshape(BD, BD, length, length, length)
            own = jnp.einsum("ijxyz,jxyz->ixyz", field.astype(jnp.float32), other.astype(jnp.float32), precision=lax.Precision.HIGHEST)
            given = jnp.einsum("ijxyz,ixyz->jxyz", field.astype(jnp.float32), mine.astype(jnp.float32), precision=lax.Precision.HIGHEST)
            return own, given.astype(jnp.bfloat16)

        own, given = lax.map(one_block, (copies, partners))
        summed = summed + own + jnp.roll(given, -round_index, axis=0).astype(jnp.float32)
    return (-summed).reshape(bands.shape)
```

```python
import functools

import jax
import jax.numpy as jnp
import numpy as np
from jax import lax
from jax.experimental import pallas as pl
from jax.experimental.pallas import tpu as pltpu
from jax.sharding import PartitionSpec as P

kernel_scale = 16.0
screen_sq = 0.05

LANES = 128
GRID = 4
OFFSETS = (1, 0, -2)
A, B, C = 0, 1, 2
MESH = pl.DeviceIdType.MESH
PLANES_AT_ONCE = 4


def dft_table(length):
    half = length // 2
    rows = np.arange(length)
    freq = np.where(rows <= half, rows, rows - half)
    phase = 2.0 * np.pi * np.outer(freq, rows) / length
    return np.where((rows <= half)[:, None], np.cos(phase), np.sin(phase))


def band_of(role, g):
    hi, lo = lax.div(g, 2), lax.rem(g, 2)
    return (hi, lo, lax.rem(hi + lo, 2))[role]


def static_band(role, g):
    return (g // 2, g % 2, (g // 2 + g % 2) % 2)[role]


def other(g, d):
    hi = lax.rem(lax.div(g, 2) + d // 2, 2)
    lo = lax.rem(lax.rem(g, 2) + d % 2, 2)
    return 2 * hi + lo


def dot(a, b):
    return jnp.dot(a, b, preferred_element_type=jnp.float32)


def kernel(n_blocks, length, planes, own_ref, fz_ref, iz_ref, r_ref, rt_ref, out_ref,
           rbuf, work, mult, acc, sendbuf, retbuf, in_send, in_recv, out_send, out_recv, local_sem):
    half = length // 2
    packed = own_ref.shape[1]
    tails = planes - packed
    me = lax.axis_index("band")
    g = lax.axis_index("grid")

    def block(offset):
        return lax.rem(me + offset + n_blocks, n_blocks)

    barrier = pltpu.get_barrier_semaphore()
    count = 0
    for offset in (-2, -1, 0, 1, 2):
        for d in range(GRID):
            if offset == 0 and d == 0:
                continue
            pl.semaphore_signal(barrier, inc=1, device_id=(block(offset), other(g, d)), device_id_type=MESH)
            count += 1

    rows = lax.broadcasted_iota(jnp.int32, (length, LANES), 0)
    cols = lax.broadcasted_iota(jnp.int32, (length, LANES), 1)

    def freq_of(i):
        return jnp.where(i <= half, i, i - half).astype(jnp.float32)

    def weight_of(i):
        return jnp.where((i == 0) | (i == half), 1.0, 2.0).astype(jnp.float32) / length

    square_ac = freq_of(rows) ** 2 + freq_of(cols) ** 2 + screen_sq
    weight_ac = weight_of(rows) * weight_of(cols) * kernel_scale

    def fill(b, _):
        bb = jnp.full((length, LANES), b, jnp.int32)
        mult[b] = weight_ac * weight_of(bb) / (square_ac + freq_of(bb) ** 2)
        return 0

    pl.semaphore_wait(barrier, count)

    def inward(role, d):
        to = other(g, d)
        return pltpu.make_async_remote_copy(
            src_ref=own_ref.at[band_of(role, to)],
            dst_ref=rbuf.at[role, g, pl.ds(0, packed)],
            send_sem=in_send.at[role, d],
            recv_sem=in_recv.at[role, d],
            device_id=(block(-OFFSETS[role]), to),
            device_id_type=MESH,
        )

    own_in = pltpu.make_async_copy(
        own_ref.at[band_of(B, g)], rbuf.at[B, g, pl.ds(0, packed)], local_sem.at[0])
    own_in.start()
    order = (3, 2, 1, 0)
    for role in (B, A, C):
        for d in order:
            if role == B and d == 0:
                continue
            inward(role, d).start()

    lax.fori_loop(0, length, fill, 0)

    lane = lax.broadcasted_iota(jnp.int32, (length, LANES), 1)

    def arrive(role, d):
        if role == B and d == 0:
            own_in.wait()
        else:
            inward(role, d).wait_recv()
        h = other(g, d)

        def unpack(q, _):
            p0 = pltpu.roll(rbuf[role, h, q].astype(jnp.float32), 32, 1)
            p1 = pltpu.roll(rbuf[role, h, tails + q].astype(jnp.float32), 64, 1)
            p2 = pltpu.roll(rbuf[role, h, 2 * tails + q].astype(jnp.float32), 96, 1)
            tail = jnp.where(lane < 32, p0, jnp.where(lane < 64, p1, p2))
            rbuf[role, h, packed + q] = tail.astype(jnp.bfloat16)
            return 0

        lax.fori_loop(0, tails, unpack, 0)

    steps = PLANES_AT_ONCE // 2

    def forward(one, two, d):
        h = other(g, d)

        def body(it, _):
            for u in range(steps):
                p = it * PLANES_AT_ONCE + 2 * u
                dens = []
                for v in range(2):
                    x = rbuf[one, h, p + v].astype(jnp.float32) * rbuf[two, h, p + v].astype(jnp.float32)
                    dens.append(x.astype(jnp.bfloat16))
                s1 = dot(jnp.concatenate(dens, axis=1), fz_ref[...]).astype(jnp.bfloat16)
                s2 = dot(r_ref[...], s1)
                for v in range(2):
                    row = pl.multiple_of((h * planes + p + v) * length, 8)
                    work[pl.ds(row, length), :] = s2[:, v * LANES:(v + 1) * LANES]
            return 0

        lax.fori_loop(0, planes // PLANES_AT_ONCE, body, 0)

    def middle():
        def body(it, _):
            for u in range(steps):
                b = it * PLANES_AT_ONCE + 2 * u
                s2 = jnp.concatenate(
                    [work[pl.ds(b + v, length, stride=length), :].astype(jnp.bfloat16) for v in range(2)], axis=1)
                m = jnp.concatenate([mult[b + v] for v in range(2)], axis=1)
                s3 = (m * dot(r_ref[...], s2)).astype(jnp.bfloat16)
                s4 = dot(rt_ref[...], s3)
                for v in range(2):
                    work[pl.ds(b + v, length, stride=length), :] = s4[:, v * LANES:(v + 1) * LANES]
            return 0

        lax.fori_loop(0, length // PLANES_AT_ONCE, body, 0)

    def backward(one, two, first_one, first_two, d):
        h = other(g, d)

        def body(it, _):
            for u in range(steps):
                p = it * PLANES_AT_ONCE + 2 * u
                s4 = []
                for v in range(2):
                    row = pl.multiple_of((h * planes + p + v) * length, 8)
                    s4.append(work[pl.ds(row, length), :].astype(jnp.bfloat16))
                s5 = dot(rt_ref[...], jnp.concatenate(s4, axis=1)).astype(jnp.bfloat16)
                pot = dot(s5, iz_ref[...]).astype(jnp.bfloat16).astype(jnp.float32)
                for v in range(2):
                    field = pot[:, v * LANES:(v + 1) * LANES]
                    for role, mate, first in ((one, two, first_one), (two, one, first_two)):
                        term = field * rbuf[mate, h, p + v].astype(jnp.float32)
                        if first:
                            acc[role, h, p + v] = term
                        else:
                            acc[role, h, p + v] += term
            return 0

        lax.fori_loop(0, planes // PLANES_AT_ONCE, body, 0)

    def outward(role, d):
        h = other(g, d)
        return pltpu.make_async_remote_copy(
            src_ref=sendbuf.at[role, h],
            dst_ref=retbuf.at[role, g],
            send_sem=out_send.at[role, d],
            recv_sem=out_recv.at[role, d],
            device_id=(block(OFFSETS[role]), h),
            device_id_type=MESH,
        )

    own_out = pltpu.make_async_copy(sendbuf.at[B, g], retbuf.at[B, g], local_sem.at[1])

    def leave(role, d):
        h = other(g, d)

        def pack(q, _):
            tail = acc[role, h, packed + q]
            for t in range(3):
                head = acc[role, h, t * tails + q]
                mixed = jnp.where(lane < 96, head, pltpu.roll(tail, 96 - 32 * t, 1))
                sendbuf[role, h, t * tails + q] = mixed.astype(jnp.bfloat16)
            return 0

        lax.fori_loop(0, tails, pack, 0)
        if role == B and d == 0:
            own_out.start()
        else:
            outward(role, d).start()

    near = (0, 1, 2, 3)
    far = (3, 2, 1, 0)
    for d in near:
        arrive(B, d)
        arrive(A, d)
        forward(A, B, d)
    middle()
    for d in far:
        backward(A, B, True, True, d)
    for d in near:
        arrive(C, d)
        forward(A, C, d)
    middle()
    for d in far:
        backward(A, C, False, True, d)
        leave(A, d)
    for d in near:
        forward(B, C, d)
    middle()
    for d in far:
        backward(B, C, False, False, d)
        leave(C, d)
        leave(B, d)

    for role in (A, B, C):
        for d in range(GRID):
            if role == B and d == 0:
                own_out.wait()
                continue
            inward(role, d).wait_send()
            outward(role, d).wait_send()
            outward(role, d).wait_recv()

    for s in range(2):
        parts = [(role, gg) for role in (A, B, C) for gg in range(GRID) if static_band(role, gg) == s]

        def add(p, _):
            total = retbuf[parts[0][0], parts[0][1], p].astype(jnp.float32)
            for role, gg in parts[1:]:
                total = total + retbuf[role, gg, p].astype(jnp.float32)
            out_ref[s, p] = -total
            return 0

        lax.fori_loop(0, packed, add, 0)


def pack_planes(x, packed):
    tails = x.shape[1] - packed
    tail = x[:, packed:]
    side = jnp.concatenate([tail[..., 32 * t:32 * t + 32] for t in range(3)], axis=1)
    assert side.shape[1] == packed and tails * 3 == packed
    return jnp.concatenate([x[:, :packed], side], axis=-1)


def unpack_planes(x, length):
    packed = x.shape[1]
    tails = packed // 3
    side = x[..., length:]
    tail = jnp.concatenate([side[:, t * tails:(t + 1) * tails] for t in range(3)], axis=-1)
    return jnp.concatenate([x[..., :length], tail], axis=1)


def per_device(n_blocks, bands):
    count, planes, length, _ = bands.shape
    assert count == 2 and length == 96 and planes * GRID == length
    packed = planes * length // LANES
    table = dft_table(length)
    pad = np.zeros((LANES, LANES))
    pad[:length, :length] = table.T
    eye = np.eye(2)
    fz = jnp.asarray(np.kron(eye, pad), jnp.bfloat16)
    iz = jnp.asarray(np.kron(eye, pad.T), jnp.bfloat16)
    r = jnp.asarray(table, jnp.bfloat16)
    rt = jnp.asarray(table.T, jnp.bfloat16)
    own = pack_planes(bands.astype(jnp.bfloat16), packed)
    vmem = pl.BlockSpec(memory_space=pltpu.VMEM)
    out = pl.pallas_call(
        functools.partial(kernel, n_blocks, length, planes),
        out_shape=jax.ShapeDtypeStruct((count, packed, length, LANES), jnp.float32),
        in_specs=[vmem] * 5,
        out_specs=vmem,
        scratch_shapes=[
            pltpu.VMEM((3, GRID, planes, length, LANES), jnp.bfloat16),
            pltpu.VMEM((length * length, LANES), jnp.float32),
            pltpu.VMEM((length, length, LANES), jnp.float32),
            pltpu.VMEM((3, GRID, planes, length, LANES), jnp.float32),
            pltpu.VMEM((3, GRID, packed, length, LANES), jnp.bfloat16),
            pltpu.VMEM((3, GRID, packed, length, LANES), jnp.bfloat16),
            pltpu.SemaphoreType.DMA((3, GRID)),
            pltpu.SemaphoreType.DMA((3, GRID)),
            pltpu.SemaphoreType.DMA((3, GRID)),
            pltpu.SemaphoreType.DMA((3, GRID)),
            pltpu.SemaphoreType.DMA((2,)),
        ],
        compiler_params=pltpu.CompilerParams(
            collective_id=0, has_side_effects=True, vmem_limit_bytes=60000 * 1024),
    )(own, fz, iz, r, rt)
    return unpack_planes(out, length)


def solution(mesh):
    n_blocks = mesh.shape["band"]
    assert mesh.shape["grid"] == GRID
    in_specs = (P("band", "grid", None, None),)
    out_specs = P("band", "grid", None, None)
    return jax.shard_map(
        functools.partial(per_device, n_blocks), mesh=mesh, in_specs=in_specs, out_specs=out_specs,
        check_vma=False,
    )
```

```python
import functools

import jax
import jax.numpy as jnp
import numpy as np
from jax import lax
from jax.experimental import pallas as pl
from jax.experimental.pallas import tpu as pltpu
from jax.sharding import PartitionSpec as P

kernel_scale = 16.0
screen_sq = 0.05

LANES = 128
GRID = 4
OFFSETS = (1, 0, -2)
A, B, C = 0, 1, 2
MESH = pl.DeviceIdType.MESH
PAD = 8
FWD, MID, BWD = 8, 16, 12


def dft_table(length):
    half = length // 2
    rows = np.arange(length)
    freq = np.where(rows <= half, rows, rows - half)
    phase = 2.0 * np.pi * np.outer(freq, rows) / length
    return np.where((rows <= half)[:, None], np.cos(phase), np.sin(phase))


def band_of(role, g):
    hi, lo = lax.div(g, 2), lax.rem(g, 2)
    return (hi, lo, lax.rem(hi + lo, 2))[role]


def static_band(role, g):
    return (g // 2, g % 2, (g // 2 + g % 2) % 2)[role]


def other(g, d):
    hi = lax.rem(lax.div(g, 2) + d // 2, 2)
    lo = lax.rem(lax.rem(g, 2) + d % 2, 2)
    return 2 * hi + lo


def dot(a, b):
    return jnp.dot(a, b, preferred_element_type=jnp.float32)


def kernel(n_blocks, length, planes, own_ref, fz_ref, iz_ref, r_ref, rt_ref, out_ref,
           rbuf, work, mult, acc, sendbuf, retbuf, in_send, in_recv, out_send, out_recv, local_sem):
    half = length // 2
    packed = own_ref.shape[1]
    tails = planes - packed
    me = lax.axis_index("band")
    g = lax.axis_index("grid")

    def block(offset):
        return lax.rem(me + offset + n_blocks, n_blocks)

    barrier = pltpu.get_barrier_semaphore()
    count = 0
    for offset in (-2, -1, 0, 1, 2):
        for d in range(GRID):
            if offset == 0 and d == 0:
                continue
            pl.semaphore_signal(barrier, inc=1, device_id=(block(offset), other(g, d)), device_id_type=MESH)
            count += 1

    rows = lax.broadcasted_iota(jnp.int32, (length, LANES), 0)
    cols = lax.broadcasted_iota(jnp.int32, (length, LANES), 1)

    def freq_of(i):
        return jnp.where(i <= half, i, i - half).astype(jnp.float32)

    def weight_of(i):
        return jnp.where((i == 0) | (i == half), 1.0, 2.0).astype(jnp.float32) / length

    square_ac = freq_of(rows) ** 2 + freq_of(cols) ** 2 + screen_sq
    weight_ac = weight_of(rows) * weight_of(cols) * kernel_scale

    def fill(b, _):
        bb = jnp.full((length, LANES), b, jnp.int32)
        mult[b] = weight_ac * weight_of(bb) / (square_ac + freq_of(bb) ** 2)
        return 0

    pl.semaphore_wait(barrier, count)

    def inward(role, d):
        to = other(g, d)
        return pltpu.make_async_remote_copy(
            src_ref=own_ref.at[band_of(role, to)],
            dst_ref=rbuf.at[role, g, pl.ds(0, packed)],
            send_sem=in_send.at[role, d],
            recv_sem=in_recv.at[role, d],
            device_id=(block(-OFFSETS[role]), to),
            device_id_type=MESH,
        )

    own_in = pltpu.make_async_copy(
        own_ref.at[band_of(B, g)], rbuf.at[B, g, pl.ds(0, packed)], local_sem.at[0])
    own_in.start()
    for d in range(GRID):
        for role in (C, A, B):
            if role == B and d == 0:
                continue
            inward(role, d).start()

    lax.fori_loop(0, length, fill, 0)

    lane = lax.broadcasted_iota(jnp.int32, (length, LANES), 1)

    def arrive(role, d):
        if role == B and d == 0:
            own_in.wait()
        else:
            inward(role, d).wait_recv()
        h = other(g, d)

        def unpack(q, _):
            p0 = pltpu.roll(rbuf[role, h, q].astype(jnp.float32), 32, 1)
            p1 = pltpu.roll(rbuf[role, h, tails + q].astype(jnp.float32), 64, 1)
            p2 = pltpu.roll(rbuf[role, h, 2 * tails + q].astype(jnp.float32), 96, 1)
            tail = jnp.where(lane < 32, p0, jnp.where(lane < 64, p1, p2))
            rbuf[role, h, packed + q] = tail.astype(jnp.bfloat16)
            return 0

        lax.fori_loop(0, tails, unpack, 0)

    def forward(one, two, d):
        h = other(g, d)

        def body(it, _):
            for u in range(FWD // 2):
                p = it * FWD + 2 * u
                dens = []
                for v in range(2):
                    x = rbuf[one, h, p + v].astype(jnp.float32) * rbuf[two, h, p + v].astype(jnp.float32)
                    dens.append(x.astype(jnp.bfloat16))
                s1 = dot(jnp.concatenate(dens, axis=1), fz_ref[...]).astype(jnp.bfloat16)
                s2 = dot(r_ref[...], s1)
                for v in range(2):
                    row = pl.multiple_of((h * planes + p + v) * (length + PAD), 8)
                    work[pl.ds(row, length), :] = s2[:, v * LANES:(v + 1) * LANES]
            return 0

        lax.fori_loop(0, planes // FWD, body, 0)

    def middle():
        def body(it, _):
            for u in range(MID // 2):
                b = it * MID + 2 * u
                s2 = jnp.concatenate(
                    [work[pl.ds(b + v, length, stride=length + PAD), :].astype(jnp.bfloat16) for v in range(2)], axis=1)
                m = jnp.concatenate([mult[b + v] for v in range(2)], axis=1)
                s3 = (m * dot(r_ref[...], s2)).astype(jnp.bfloat16)
                s4 = dot(rt_ref[...], s3)
                for v in range(2):
                    work[pl.ds(b + v, length, stride=length + PAD), :] = s4[:, v * LANES:(v + 1) * LANES]
            return 0

        lax.fori_loop(0, length // MID, body, 0)

    def backward(one, two, first_one, first_two, d):
        h = other(g, d)

        def body(it, _):
            for u in range(BWD // 2):
                p = it * BWD + 2 * u
                s4 = []
                for v in range(2):
                    row = pl.multiple_of((h * planes + p + v) * (length + PAD), 8)
                    s4.append(work[pl.ds(row, length), :].astype(jnp.bfloat16))
                s5 = dot(rt_ref[...], jnp.concatenate(s4, axis=1)).astype(jnp.bfloat16)
                pot = dot(s5, iz_ref[...]).astype(jnp.bfloat16).astype(jnp.float32)
                for v in range(2):
                    field = pot[:, v * LANES:(v + 1) * LANES]
                    for role, mate, first in ((one, two, first_one), (two, one, first_two)):
                        term = field * rbuf[mate, h, p + v].astype(jnp.float32)
                        if first:
                            acc[role, h, p + v] = term
                        else:
                            acc[role, h, p + v] += term
            return 0

        lax.fori_loop(0, planes // BWD, body, 0)

    def outward(role, d):
        h = other(g, d)
        return pltpu.make_async_remote_copy(
            src_ref=sendbuf.at[role, h],
            dst_ref=retbuf.at[role, g],
            send_sem=out_send.at[role, d],
            recv_sem=out_recv.at[role, d],
            device_id=(block(OFFSETS[role]), h),
            device_id_type=MESH,
        )

    own_out = pltpu.make_async_copy(sendbuf.at[B, g], retbuf.at[B, g], local_sem.at[1])

    def leave(role, d):
        h = other(g, d)

        def pack(q, _):
            tail = acc[role, h, packed + q]
            for t in range(3):
                head = acc[role, h, t * tails + q]
                mixed = jnp.where(lane < 96, head, pltpu.roll(tail, 96 - 32 * t, 1))
                sendbuf[role, h, t * tails + q] = mixed.astype(jnp.bfloat16)
            return 0

        lax.fori_loop(0, tails, pack, 0)
        if role == B and d == 0:
            own_out.start()
        else:
            outward(role, d).start()

    near = (0, 1, 2, 3)
    far = (3, 2, 1, 0)
    for d in near:
        arrive(B, d)
        arrive(A, d)
        forward(A, B, d)
    middle()
    for d in far:
        backward(A, B, True, True, d)
    for d in near:
        arrive(C, d)
        forward(A, C, d)
    middle()
    for d in far:
        backward(A, C, False, True, d)
        leave(A, d)
    for d in near:
        forward(B, C, d)
    middle()
    for d in far:
        backward(B, C, False, False, d)
        leave(C, d)
        leave(B, d)

    for role in (A, B, C):
        for d in range(GRID):
            if role == B and d == 0:
                own_out.wait()
                continue
            inward(role, d).wait_send()
            outward(role, d).wait_send()
            outward(role, d).wait_recv()

    for s in range(2):
        parts = [(role, gg) for role in (A, B, C) for gg in range(GRID) if static_band(role, gg) == s]

        def add(p, _):
            total = retbuf[parts[0][0], parts[0][1], p].astype(jnp.float32)
            for role, gg in parts[1:]:
                total = total + retbuf[role, gg, p].astype(jnp.float32)
            out_ref[s, p] = -total
            return 0

        lax.fori_loop(0, packed, add, 0)


def pack_planes(x, packed):
    tails = x.shape[1] - packed
    tail = x[:, packed:]
    side = jnp.concatenate([tail[..., 32 * t:32 * t + 32] for t in range(3)], axis=1)
    assert side.shape[1] == packed and tails * 3 == packed
    return jnp.concatenate([x[:, :packed], side], axis=-1)


def unpack_planes(x, length):
    packed = x.shape[1]
    tails = packed // 3
    side = x[..., length:]
    tail = jnp.concatenate([side[:, t * tails:(t + 1) * tails] for t in range(3)], axis=-1)
    return jnp.concatenate([x[..., :length], tail], axis=1)


def per_device(n_blocks, bands):
    count, planes, length, _ = bands.shape
    assert count == 2 and length == 96 and planes * GRID == length
    packed = planes * length // LANES
    table = dft_table(length)
    pad = np.zeros((LANES, LANES))
    pad[:length, :length] = table.T
    eye = np.eye(2)
    fz = jnp.asarray(np.kron(eye, pad), jnp.bfloat16)
    iz = jnp.asarray(np.kron(eye, pad.T), jnp.bfloat16)
    r = jnp.asarray(table, jnp.bfloat16)
    rt = jnp.asarray(table.T, jnp.bfloat16)
    own = pack_planes(bands.astype(jnp.bfloat16), packed)
    vmem = pl.BlockSpec(memory_space=pltpu.VMEM)
    out = pl.pallas_call(
        functools.partial(kernel, n_blocks, length, planes),
        out_shape=jax.ShapeDtypeStruct((count, packed, length, LANES), jnp.float32),
        in_specs=[vmem] * 5,
        out_specs=vmem,
        scratch_shapes=[
            pltpu.VMEM((3, GRID, planes, length, LANES), jnp.bfloat16),
            pltpu.VMEM((length * (length + PAD), LANES), jnp.float32),
            pltpu.VMEM((length, length, LANES), jnp.float32),
            pltpu.VMEM((3, GRID, planes, length, LANES), jnp.float32),
            pltpu.VMEM((3, GRID, packed, length, LANES), jnp.bfloat16),
            pltpu.VMEM((3, GRID, packed, length, LANES), jnp.bfloat16),
            pltpu.SemaphoreType.DMA((3, GRID)),
            pltpu.SemaphoreType.DMA((3, GRID)),
            pltpu.SemaphoreType.DMA((3, GRID)),
            pltpu.SemaphoreType.DMA((3, GRID)),
            pltpu.SemaphoreType.DMA((2,)),
        ],
        compiler_params=pltpu.CompilerParams(
            collective_id=0, has_side_effects=True, vmem_limit_bytes=60000 * 1024),
    )(own, fz, iz, r, rt)
    return unpack_planes(out, length)


def solution(mesh):
    n_blocks = mesh.shape["band"]
    assert mesh.shape["grid"] == GRID
    in_specs = (P("band", "grid", None, None),)
    out_specs = P("band", "grid", None, None)
    return jax.shard_map(
        functools.partial(per_device, n_blocks), mesh=mesh, in_specs=in_specs, out_specs=out_specs,
        check_vma=False,
    )
```

```python
import functools

import jax
import jax.numpy as jnp
import numpy as np
from jax import lax
from jax.experimental import pallas as pl
from jax.experimental.pallas import tpu as pltpu
from jax.sharding import PartitionSpec as P

kernel_scale = 16.0
screen_sq = 0.05

LANES = 128
GRID = 4
OFFSETS = (1, 0, -2)
A, B, C = 0, 1, 2
MESH = pl.DeviceIdType.MESH
PAD = 8
FWD, MID, BWD = 8, 16, 12


def dft_table(length):
    half = length // 2
    rows = np.arange(length)
    freq = np.where(rows <= half, rows, rows - half)
    phase = 2.0 * np.pi * np.outer(freq, rows) / length
    return np.where((rows <= half)[:, None], np.cos(phase), np.sin(phase))


def band_of(role, g):
    hi, lo = lax.div(g, 2), lax.rem(g, 2)
    return (lax.rem(hi + lo, 2), lo, hi)[role]


def static_band(role, g):
    return ((g // 2 + g % 2) % 2, g % 2, g // 2)[role]


def other(g, d):
    hi = lax.rem(lax.div(g, 2) + d // 2, 2)
    lo = lax.rem(lax.rem(g, 2) + d % 2, 2)
    return 2 * hi + lo


def dot(a, b):
    return jnp.dot(a, b, preferred_element_type=jnp.float32)


def kernel(n_blocks, length, planes, own_ref, fz_ref, iz_ref, r_ref, rt_ref, out_ref,
           rbuf, work, mult, acc, sendbuf, retbuf, presum, in_send, in_recv, out_send, out_recv, local_sem):
    half = length // 2
    packed = own_ref.shape[1]
    tails = planes - packed
    me = lax.axis_index("band")
    g = lax.axis_index("grid")

    def block(offset):
        return lax.rem(me + offset + n_blocks, n_blocks)

    barrier = pltpu.get_barrier_semaphore()
    count = 0
    for offset in (-2, -1, 0, 1, 2):
        for d in range(GRID):
            if offset == 0 and d == 0:
                continue
            pl.semaphore_signal(barrier, inc=1, device_id=(block(offset), other(g, d)), device_id_type=MESH)
            count += 1

    rows = lax.broadcasted_iota(jnp.int32, (length, LANES), 0)
    cols = lax.broadcasted_iota(jnp.int32, (length, LANES), 1)

    def freq_of(i):
        return jnp.where(i <= half, i, i - half).astype(jnp.float32)

    def weight_of(i):
        return jnp.where((i == 0) | (i == half), 1.0, 2.0).astype(jnp.float32) / length

    square_ac = freq_of(rows) ** 2 + freq_of(cols) ** 2 + screen_sq
    weight_ac = weight_of(rows) * weight_of(cols) * kernel_scale

    def fill(b, _):
        bb = jnp.full((length, LANES), b, jnp.int32)
        mult[b] = weight_ac * weight_of(bb) / (square_ac + freq_of(bb) ** 2)
        return 0

    pl.semaphore_wait(barrier, count)

    def inward(role, d):
        to = other(g, d)
        return pltpu.make_async_remote_copy(
            src_ref=own_ref.at[band_of(role, to)],
            dst_ref=rbuf.at[role, g, pl.ds(0, packed)],
            send_sem=in_send.at[role, d],
            recv_sem=in_recv.at[role, d],
            device_id=(block(-OFFSETS[role]), to),
            device_id_type=MESH,
        )

    own_in = pltpu.make_async_copy(
        own_ref.at[band_of(B, g)], rbuf.at[B, g, pl.ds(0, packed)], local_sem.at[0])
    own_in.start()
    for d in range(GRID):
        for role in (A, B, C):
            if (role == B and d == 0) or (role == C and d % 2 == 1):
                continue
            inward(role, d).start()

    lax.fori_loop(0, length, fill, 0)

    lane = lax.broadcasted_iota(jnp.int32, (length, LANES), 1)

    def relay(d):
        h = other(g, d)
        return pltpu.make_async_remote_copy(
            src_ref=rbuf.at[C, h, pl.ds(0, packed)],
            dst_ref=rbuf.at[C, h, pl.ds(0, packed)],
            send_sem=in_send.at[C, d + 1],
            recv_sem=in_recv.at[C, d + 1],
            device_id=(me, other(g, 1)),
            device_id_type=MESH,
        )

    def arrive(role, d):
        if role == B and d == 0:
            own_in.wait()
        elif role == C and d % 2 == 1:
            relay(d - 1).wait_recv()
        else:
            inward(role, d).wait_recv()
            if role == C:
                relay(d).start()
        h = other(g, d)

        def unpack(q, _):
            p0 = pltpu.roll(rbuf[role, h, q].astype(jnp.float32), 32, 1)
            p1 = pltpu.roll(rbuf[role, h, tails + q].astype(jnp.float32), 64, 1)
            p2 = pltpu.roll(rbuf[role, h, 2 * tails + q].astype(jnp.float32), 96, 1)
            tail = jnp.where(lane < 32, p0, jnp.where(lane < 64, p1, p2))
            rbuf[role, h, packed + q] = tail.astype(jnp.bfloat16)
            return 0

        lax.fori_loop(0, tails, unpack, 0)

    def forward(one, two, d):
        h = other(g, d)

        def body(it, _):
            for u in range(FWD // 2):
                p = it * FWD + 2 * u
                dens = []
                for v in range(2):
                    x = rbuf[one, h, p + v].astype(jnp.float32) * rbuf[two, h, p + v].astype(jnp.float32)
                    dens.append(x.astype(jnp.bfloat16))
                s1 = dot(jnp.concatenate(dens, axis=1), fz_ref[...]).astype(jnp.bfloat16)
                s2 = dot(r_ref[...], s1)
                for v in range(2):
                    row = pl.multiple_of((h * planes + p + v) * (length + PAD), 8)
                    work[pl.ds(row, length), :] = s2[:, v * LANES:(v + 1) * LANES]
            return 0

        lax.fori_loop(0, planes // FWD, body, 0)

    def middle():
        def body(it, _):
            for u in range(MID // 2):
                b = it * MID + 2 * u
                s2 = jnp.concatenate(
                    [work[pl.ds(b + v, length, stride=length + PAD), :].astype(jnp.bfloat16) for v in range(2)], axis=1)
                m = jnp.concatenate([mult[b + v] for v in range(2)], axis=1)
                s3 = (m * dot(r_ref[...], s2)).astype(jnp.bfloat16)
                s4 = dot(rt_ref[...], s3)
                for v in range(2):
                    work[pl.ds(b + v, length, stride=length + PAD), :] = s4[:, v * LANES:(v + 1) * LANES]
            return 0

        lax.fori_loop(0, length // MID, body, 0)

    def backward(one, two, first_one, first_two, d):
        h = other(g, d)

        def body(it, _):
            for u in range(BWD // 2):
                p = it * BWD + 2 * u
                s4 = []
                for v in range(2):
                    row = pl.multiple_of((h * planes + p + v) * (length + PAD), 8)
                    s4.append(work[pl.ds(row, length), :].astype(jnp.bfloat16))
                s5 = dot(rt_ref[...], jnp.concatenate(s4, axis=1)).astype(jnp.bfloat16)
                pot = dot(s5, iz_ref[...]).astype(jnp.bfloat16).astype(jnp.float32)
                for v in range(2):
                    field = pot[:, v * LANES:(v + 1) * LANES]
                    for role, mate, first in ((one, two, first_one), (two, one, first_two)):
                        term = field * rbuf[mate, h, p + v].astype(jnp.float32)
                        if first:
                            acc[role, h, p + v] = term
                        else:
                            acc[role, h, p + v] += term
            return 0

        lax.fori_loop(0, planes // BWD, body, 0)

    def outward(role, d):
        h = other(g, d)
        return pltpu.make_async_remote_copy(
            src_ref=sendbuf.at[role, h],
            dst_ref=retbuf.at[role, g],
            send_sem=out_send.at[role, d],
            recv_sem=out_recv.at[role, d],
            device_id=(block(OFFSETS[role]), h),
            device_id_type=MESH,
        )

    def exchange(d):
        h = other(g, d)
        return pltpu.make_async_remote_copy(
            src_ref=sendbuf.at[C, h],
            dst_ref=presum.at[d // 2],
            send_sem=out_send.at[C, d],
            recv_sem=out_recv.at[C, d],
            device_id=(me, other(g, 1)),
            device_id_type=MESH,
        )

    own_out = pltpu.make_async_copy(sendbuf.at[B, g], retbuf.at[B, g], local_sem.at[1])

    def leave(role, d):
        h = other(g, d)
        joined = role == C and d % 2 == 0
        if joined:
            exchange(d + 1).wait_recv()

        def pack(q, _):
            tail = acc[role, h, packed + q]
            for t in range(3):
                head = acc[role, h, t * tails + q]
                mixed = jnp.where(lane < 96, head, pltpu.roll(tail, 96 - 32 * t, 1))
                if joined:
                    mixed = mixed + presum[d // 2, t * tails + q].astype(jnp.float32)
                sendbuf[role, h, t * tails + q] = mixed.astype(jnp.bfloat16)
            return 0

        lax.fori_loop(0, tails, pack, 0)
        if role == B and d == 0:
            own_out.start()
        elif role == C and d % 2 == 1:
            exchange(d).start()
        else:
            outward(role, d).start()

    near = (0, 1, 2, 3)
    far = (3, 2, 1, 0)
    for d in near:
        arrive(B, d)
        arrive(A, d)
        forward(A, B, d)
    middle()
    for d in far:
        backward(A, B, True, True, d)
    for d in (0, 2, 1, 3):
        arrive(C, d)
        forward(A, C, d)
    middle()
    for d in far:
        backward(A, C, False, True, d)
        leave(A, d)
    for d in near:
        forward(B, C, d)
    middle()
    for d in (3, 1, 2, 0):
        backward(B, C, False, False, d)
        leave(C, d)
        leave(B, d)

    for role in (A, B, C):
        for d in range(GRID):
            if role == B and d == 0:
                own_out.wait()
                continue
            if role == C and d % 2 == 1:
                relay(d - 1).wait_send()
                exchange(d).wait_send()
                continue
            inward(role, d).wait_send()
            outward(role, d).wait_send()
            outward(role, d).wait_recv()

    for s in range(2):
        parts = [(role, gg) for role in (A, B) for gg in range(GRID) if static_band(role, gg) == s]
        parts.append((C, 2 * s + lax.rem(g, 2)))

        def add(p, _):
            total = retbuf[parts[0][0], parts[0][1], p].astype(jnp.float32)
            for role, gg in parts[1:]:
                total = total + retbuf[role, gg, p].astype(jnp.float32)
            out_ref[s, p] = -total
            return 0

        lax.fori_loop(0, packed, add, 0)


def pack_planes(x, packed):
    tails = x.shape[1] - packed
    tail = x[:, packed:]
    side = jnp.concatenate([tail[..., 32 * t:32 * t + 32] for t in range(3)], axis=1)
    assert side.shape[1] == packed and tails * 3 == packed
    return jnp.concatenate([x[:, :packed], side], axis=-1)


def unpack_planes(x, length):
    packed = x.shape[1]
    tails = packed // 3
    side = x[..., length:]
    tail = jnp.concatenate([side[:, t * tails:(t + 1) * tails] for t in range(3)], axis=-1)
    return jnp.concatenate([x[..., :length], tail], axis=1)


def per_device(n_blocks, bands):
    count, planes, length, _ = bands.shape
    assert count == 2 and length == 96 and planes * GRID == length
    packed = planes * length // LANES
    table = dft_table(length)
    pad = np.zeros((LANES, LANES))
    pad[:length, :length] = table.T
    eye = np.eye(2)
    fz = jnp.asarray(np.kron(eye, pad), jnp.bfloat16)
    iz = jnp.asarray(np.kron(eye, pad.T), jnp.bfloat16)
    r = jnp.asarray(table, jnp.bfloat16)
    rt = jnp.asarray(table.T, jnp.bfloat16)
    own = pack_planes(bands.astype(jnp.bfloat16), packed)
    vmem = pl.BlockSpec(memory_space=pltpu.VMEM)
    out = pl.pallas_call(
        functools.partial(kernel, n_blocks, length, planes),
        out_shape=jax.ShapeDtypeStruct((count, packed, length, LANES), jnp.float32),
        in_specs=[vmem] * 5,
        out_specs=vmem,
        scratch_shapes=[
            pltpu.VMEM((3, GRID, planes, length, LANES), jnp.bfloat16),
            pltpu.VMEM((length * (length + PAD), LANES), jnp.float32),
            pltpu.VMEM((length, length, LANES), jnp.float32),
            pltpu.VMEM((3, GRID, planes, length, LANES), jnp.float32),
            pltpu.VMEM((3, GRID, packed, length, LANES), jnp.bfloat16),
            pltpu.VMEM((3, GRID, packed, length, LANES), jnp.bfloat16),
            pltpu.VMEM((GRID // 2, packed, length, LANES), jnp.bfloat16),
            pltpu.SemaphoreType.DMA((3, GRID)),
            pltpu.SemaphoreType.DMA((3, GRID)),
            pltpu.SemaphoreType.DMA((3, GRID)),
            pltpu.SemaphoreType.DMA((3, GRID)),
            pltpu.SemaphoreType.DMA((2,)),
        ],
        compiler_params=pltpu.CompilerParams(
            collective_id=0, has_side_effects=True, vmem_limit_bytes=60000 * 1024),
    )(own, fz, iz, r, rt)
    return unpack_planes(out, length)


def solution(mesh):
    n_blocks = mesh.shape["band"]
    assert mesh.shape["grid"] == GRID
    in_specs = (P("band", "grid", None, None),)
    out_specs = P("band", "grid", None, None)
    return jax.shard_map(
        functools.partial(per_device, n_blocks), mesh=mesh, in_specs=in_specs, out_specs=out_specs,
        check_vma=False,
    )
```

```python
import functools

import jax
import jax.numpy as jnp
import numpy as np
from jax import lax
from jax.experimental import pallas as pl
from jax.experimental.pallas import tpu as pltpu
from jax.sharding import PartitionSpec as P

kernel_scale = 16.0
screen_sq = 0.05

LANES = 128
GRID = 4
OFFSETS = (1, 0, -2)
A, B, C = 0, 1, 2
MESH = pl.DeviceIdType.MESH
PAD = 8
FWD, MID, BWD = 8, 16, 12


def dft_table(length):
    half = length // 2
    rows = np.arange(length)
    freq = np.where(rows <= half, rows, rows - half)
    phase = 2.0 * np.pi * np.outer(freq, rows) / length
    return np.where((rows <= half)[:, None], np.cos(phase), np.sin(phase))


def band_of(role, g):
    hi, lo = lax.div(g, 2), lax.rem(g, 2)
    return (lax.rem(hi + lo, 2), lo, hi)[role]


def static_band(role, g):
    return ((g // 2 + g % 2) % 2, g % 2, g // 2)[role]


def other(g, d):
    hi = lax.rem(lax.div(g, 2) + d // 2, 2)
    lo = lax.rem(lax.rem(g, 2) + d % 2, 2)
    return 2 * hi + lo


def dot(a, b):
    return jnp.dot(a, b, preferred_element_type=jnp.float32)


def kernel(n_blocks, length, planes, own_ref, fz_ref, iz_ref, r_ref, rt_ref, out_ref,
           rbuf, work, mult, acc, sendbuf, retbuf, presum, in_send, in_recv, out_send, out_recv, local_sem):
    half = length // 2
    packed = own_ref.shape[1]
    tails = planes - packed
    me = lax.axis_index("band")
    g = lax.axis_index("grid")

    def block(offset):
        return lax.rem(me + offset + n_blocks, n_blocks)

    barrier = pltpu.get_barrier_semaphore()
    count = 0
    for offset in (-2, -1, 0, 1, 2):
        for d in range(GRID):
            if offset == 0 and d == 0:
                continue
            pl.semaphore_signal(barrier, inc=1, device_id=(block(offset), other(g, d)), device_id_type=MESH)
            count += 1

    rows = lax.broadcasted_iota(jnp.int32, (length, LANES), 0)
    cols = lax.broadcasted_iota(jnp.int32, (length, LANES), 1)

    def freq_of(i):
        return jnp.where(i <= half, i, i - half).astype(jnp.float32)

    def weight_of(i):
        return jnp.where((i == 0) | (i == half), 1.0, 2.0).astype(jnp.float32) / length

    square_ac = freq_of(rows) ** 2 + freq_of(cols) ** 2 + screen_sq
    weight_ac = weight_of(rows) * weight_of(cols) * kernel_scale

    def fill(b, _):
        bb = jnp.full((length, LANES), b, jnp.int32)
        mult[b] = weight_ac * weight_of(bb) / (square_ac + freq_of(bb) ** 2)
        return 0

    pl.semaphore_wait(barrier, count)

    def inward(role, d):
        to = other(g, d)
        return pltpu.make_async_remote_copy(
            src_ref=own_ref.at[band_of(role, to)],
            dst_ref=rbuf.at[role, g, pl.ds(0, packed)],
            send_sem=in_send.at[role, d],
            recv_sem=in_recv.at[role, d],
            device_id=(block(-OFFSETS[role]), to),
            device_id_type=MESH,
        )

    own_in = pltpu.make_async_copy(
        own_ref.at[band_of(B, g)], rbuf.at[B, g, pl.ds(0, packed)], local_sem.at[0])
    own_in.start()
    for d in range(GRID):
        for role in (A, B):
            if role == B and d == 0:
                continue
            inward(role, d).start()

    lax.fori_loop(0, length, fill, 0)

    lane = lax.broadcasted_iota(jnp.int32, (length, LANES), 1)

    def relay(d):
        h = other(g, d)
        return pltpu.make_async_remote_copy(
            src_ref=rbuf.at[C, h, pl.ds(0, packed)],
            dst_ref=rbuf.at[C, h, pl.ds(0, packed)],
            send_sem=in_send.at[C, d + 1],
            recv_sem=in_recv.at[C, d + 1],
            device_id=(me, other(g, 1)),
            device_id_type=MESH,
        )

    def arrive(role, d):
        if role == B and d == 0:
            own_in.wait()
        elif role == C and d % 2 == 1:
            relay(d - 1).wait_recv()
        else:
            inward(role, d).wait_recv()
            if role == C:
                relay(d).start()
        h = other(g, d)

        def unpack(q, _):
            p0 = pltpu.roll(rbuf[role, h, q].astype(jnp.float32), 32, 1)
            p1 = pltpu.roll(rbuf[role, h, tails + q].astype(jnp.float32), 64, 1)
            p2 = pltpu.roll(rbuf[role, h, 2 * tails + q].astype(jnp.float32), 96, 1)
            tail = jnp.where(lane < 32, p0, jnp.where(lane < 64, p1, p2))
            rbuf[role, h, packed + q] = tail.astype(jnp.bfloat16)
            return 0

        lax.fori_loop(0, tails, unpack, 0)

    def forward(one, two, d):
        h = other(g, d)

        def body(it, _):
            for u in range(FWD // 2):
                p = it * FWD + 2 * u
                dens = []
                for v in range(2):
                    x = rbuf[one, h, p + v].astype(jnp.float32) * rbuf[two, h, p + v].astype(jnp.float32)
                    dens.append(x.astype(jnp.bfloat16))
                s1 = dot(jnp.concatenate(dens, axis=1), fz_ref[...]).astype(jnp.bfloat16)
                s2 = dot(r_ref[...], s1)
                for v in range(2):
                    row = pl.multiple_of((h * planes + p + v) * (length + PAD), 8)
                    work[pl.ds(row, length), :] = s2[:, v * LANES:(v + 1) * LANES]
            return 0

        lax.fori_loop(0, planes // FWD, body, 0)

    def middle():
        def body(it, _):
            for u in range(MID // 2):
                b = it * MID + 2 * u
                s2 = jnp.concatenate(
                    [work[pl.ds(b + v, length, stride=length + PAD), :].astype(jnp.bfloat16) for v in range(2)], axis=1)
                m = jnp.concatenate([mult[b + v] for v in range(2)], axis=1)
                s3 = (m * dot(r_ref[...], s2)).astype(jnp.bfloat16)
                s4 = dot(rt_ref[...], s3)
                for v in range(2):
                    work[pl.ds(b + v, length, stride=length + PAD), :] = s4[:, v * LANES:(v + 1) * LANES]
            return 0

        lax.fori_loop(0, length // MID, body, 0)

    def backward(one, two, first_one, first_two, d):
        h = other(g, d)

        def body(it, _):
            for u in range(BWD // 2):
                p = it * BWD + 2 * u
                s4 = []
                for v in range(2):
                    row = pl.multiple_of((h * planes + p + v) * (length + PAD), 8)
                    s4.append(work[pl.ds(row, length), :].astype(jnp.bfloat16))
                s5 = dot(rt_ref[...], jnp.concatenate(s4, axis=1)).astype(jnp.bfloat16)
                pot = dot(s5, iz_ref[...]).astype(jnp.bfloat16).astype(jnp.float32)
                for v in range(2):
                    field = pot[:, v * LANES:(v + 1) * LANES]
                    for role, mate, first in ((one, two, first_one), (two, one, first_two)):
                        term = field * rbuf[mate, h, p + v].astype(jnp.float32)
                        if first:
                            acc[role, h, p + v] = term
                        else:
                            acc[role, h, p + v] += term
            return 0

        lax.fori_loop(0, planes // BWD, body, 0)

    def outward(role, d):
        h = other(g, d)
        return pltpu.make_async_remote_copy(
            src_ref=sendbuf.at[role, h],
            dst_ref=retbuf.at[role, g],
            send_sem=out_send.at[role, d],
            recv_sem=out_recv.at[role, d],
            device_id=(block(OFFSETS[role]), h),
            device_id_type=MESH,
        )

    def exchange(d):
        h = other(g, d)
        return pltpu.make_async_remote_copy(
            src_ref=sendbuf.at[C, h],
            dst_ref=presum.at[d // 2],
            send_sem=out_send.at[C, d],
            recv_sem=out_recv.at[C, d],
            device_id=(me, other(g, 1)),
            device_id_type=MESH,
        )

    own_out = pltpu.make_async_copy(sendbuf.at[B, g], retbuf.at[B, g], local_sem.at[1])

    def leave(role, d):
        h = other(g, d)
        joined = role == C and d % 2 == 0
        if joined:
            exchange(d + 1).wait_recv()

        def pack(q, _):
            tail = acc[role, h, packed + q]
            for t in range(3):
                head = acc[role, h, t * tails + q]
                mixed = jnp.where(lane < 96, head, pltpu.roll(tail, 96 - 32 * t, 1))
                if joined:
                    mixed = mixed + presum[d // 2, t * tails + q].astype(jnp.float32)
                sendbuf[role, h, t * tails + q] = mixed.astype(jnp.bfloat16)
            return 0

        lax.fori_loop(0, tails, pack, 0)
        if role == B and d == 0:
            own_out.start()
        elif role == C and d % 2 == 1:
            exchange(d).start()
        else:
            outward(role, d).start()

    near = (0, 1, 2, 3)
    far = (3, 2, 1, 0)
    for d in near:
        arrive(B, d)
        arrive(A, d)
        if d == 2:
            for c in (0, 2):
                inward(C, c).start()
        forward(A, B, d)
    middle()
    for d in far:
        backward(A, B, True, True, d)
    for d in (0, 2, 1, 3):
        arrive(C, d)
        forward(A, C, d)
    middle()
    for d in far:
        backward(A, C, False, True, d)
        leave(A, d)
    for d in near:
        forward(B, C, d)
    middle()
    for d in (3, 1, 2, 0):
        backward(B, C, False, False, d)
        leave(C, d)
        leave(B, d)

    for role in (A, B, C):
        for d in range(GRID):
            if role == B and d == 0:
                own_out.wait()
                continue
            if role == C and d % 2 == 1:
                relay(d - 1).wait_send()
                exchange(d).wait_send()
                continue
            inward(role, d).wait_send()
            outward(role, d).wait_send()
            outward(role, d).wait_recv()

    for s in range(2):
        parts = [(role, gg) for role in (A, B) for gg in range(GRID) if static_band(role, gg) == s]
        parts.append((C, 2 * s + lax.rem(g, 2)))

        def add(p, _):
            total = retbuf[parts[0][0], parts[0][1], p].astype(jnp.float32)
            for role, gg in parts[1:]:
                total = total + retbuf[role, gg, p].astype(jnp.float32)
            out_ref[s, p] = -total
            return 0

        lax.fori_loop(0, packed, add, 0)


def pack_planes(x, packed):
    tails = x.shape[1] - packed
    tail = x[:, packed:]
    side = jnp.concatenate([tail[..., 32 * t:32 * t + 32] for t in range(3)], axis=1)
    assert side.shape[1] == packed and tails * 3 == packed
    return jnp.concatenate([x[:, :packed], side], axis=-1)


def unpack_planes(x, length):
    packed = x.shape[1]
    tails = packed // 3
    side = x[..., length:]
    tail = jnp.concatenate([side[:, t * tails:(t + 1) * tails] for t in range(3)], axis=-1)
    return jnp.concatenate([x[..., :length], tail], axis=1)


def per_device(n_blocks, bands):
    count, planes, length, _ = bands.shape
    assert count == 2 and length == 96 and planes * GRID == length
    packed = planes * length // LANES
    table = dft_table(length)
    pad = np.zeros((LANES, LANES))
    pad[:length, :length] = table.T
    eye = np.eye(2)
    fz = jnp.asarray(np.kron(eye, pad), jnp.bfloat16)
    iz = jnp.asarray(np.kron(eye, pad.T), jnp.bfloat16)
    r = jnp.asarray(table, jnp.bfloat16)
    rt = jnp.asarray(table.T, jnp.bfloat16)
    own = pack_planes(bands.astype(jnp.bfloat16), packed)
    vmem = pl.BlockSpec(memory_space=pltpu.VMEM)
    out = pl.pallas_call(
        functools.partial(kernel, n_blocks, length, planes),
        out_shape=jax.ShapeDtypeStruct((count, packed, length, LANES), jnp.float32),
        in_specs=[vmem] * 5,
        out_specs=vmem,
        scratch_shapes=[
            pltpu.VMEM((3, GRID, planes, length, LANES), jnp.bfloat16),
            pltpu.VMEM((length * (length + PAD), LANES), jnp.float32),
            pltpu.VMEM((length, length, LANES), jnp.float32),
            pltpu.VMEM((3, GRID, planes, length, LANES), jnp.float32),
            pltpu.VMEM((3, GRID, packed, length, LANES), jnp.bfloat16),
            pltpu.VMEM((3, GRID, packed, length, LANES), jnp.bfloat16),
            pltpu.VMEM((GRID // 2, packed, length, LANES), jnp.bfloat16),
            pltpu.SemaphoreType.DMA((3, GRID)),
            pltpu.SemaphoreType.DMA((3, GRID)),
            pltpu.SemaphoreType.DMA((3, GRID)),
            pltpu.SemaphoreType.DMA((3, GRID)),
            pltpu.SemaphoreType.DMA((2,)),
        ],
        compiler_params=pltpu.CompilerParams(
            collective_id=0, has_side_effects=True, vmem_limit_bytes=60000 * 1024),
    )(own, fz, iz, r, rt)
    return unpack_planes(out, length)


def solution(mesh):
    n_blocks = mesh.shape["band"]
    assert mesh.shape["grid"] == GRID
    in_specs = (P("band", "grid", None, None),)
    out_specs = P("band", "grid", None, None)
    return jax.shard_map(
        functools.partial(per_device, n_blocks), mesh=mesh, in_specs=in_specs, out_specs=out_specs,
        check_vma=False,
    )
```
